32 devices in a mesh: section: 4 (over y, core), lat: 2 (over x), lon: 4 (over z).
Axes of the slice: x: 2, y: 2, z: 4, core: 2. Of those that a mesh axis runs over, the one named last changes fastest.
Arguments:
- tokens: bfloat16 [4, 16, 64, 1536], P('section', 'lat', 'lon'), may hold values from -6 to 6
- grad_out: bfloat16 [4, 16, 64, 1536], P('section', 'lat', 'lon'), may hold values from -6 to 6
- gain: bfloat16 [4, 1536], P('section'), may hold values from 0.099609375 to 1.8984375
- w_in: bfloat16 [4, 3, 1536, 768], P('section', None, 'lon'), may hold values from -0.16585087 to 0.16585087
- w_out: bfloat16 [4, 1536, 768], P('section', 'lon'), may hold values from -0.21875 to 0.21875
Outputs:
- passed: bfloat16 [4, 16, 64, 1536], P('section', 'lat', 'lon')
The draws below stay inside these ranges and needn't reach their ends.
All inputs are finite; a program needn't handle non-finite values.
Results may differ from the reference program's by a relative error of at most 0.0052.
Values may be sent and summed in bfloat16 or wider, within the bound.
No kernel may reach another device: no remote copies, remote signals or barrier semaphores. Data moves between devices by JAX's collectives and lax.ppermute only.
A program may use at most 64 MiB of HBM per device.

```python
import jax
import jax.numpy as jnp
from jax import lax

D = 1536
HEADS = 8
HEAD = 96
INNER = 768
RADIUS = 6
ROWS_DEV = 8
COLS_DEV = 16
SECTIONS = 4
NLAT = 16
NLON = 64
N_SECTION = 4
N_LAT = 2
N_LON = 4


shared_strength = 1.4


def shared_signs(key):
    return jax.random.rademacher(jax.random.fold_in(key, 7101), (SECTIONS, D), dtype=jnp.float32)


def inner_signs(key):
    return jax.random.rademacher(jax.random.fold_in(key, 7103), (SECTIONS, INNER), dtype=jnp.float32)


def draw_tokens(key, part):
    noise_key, level_key, offset_key = jax.random.split(jax.random.fold_in(key, 7102), 3)
    shape = (SECTIONS, NLAT, NLON, D)
    noise = jax.random.normal(noise_key, shape, jnp.float32)
    levels = jax.random.uniform(level_key, (SECTIONS, NLAT, NLON, 1), jnp.float32, 0.6, 1.0)
    offsets = jax.random.randint(offset_key, (SECTIONS, 2), 0, 16)
    rows = jnp.arange(NLAT, dtype=jnp.int32)[None, :, None]
    cols = jnp.arange(NLON, dtype=jnp.int32)[None, None, :]
    planted = ((rows + offsets[:, 0][:, None, None]) % 8 < 2) & ((cols + offsets[:, 1][:, None, None]) % 16 < 3)
    signs = shared_signs(key)[:, None, None, :]
    aligned = levels * signs + jnp.sqrt(1.0 - levels * levels) * noise
    mixed = jnp.where(planted[:, :, :, None], aligned, noise)
    return jnp.clip(mixed, -6.0, 6.0).astype(jnp.bfloat16)


def draw_w_in(key, part):
    base_key = jax.random.fold_in(key, 7104)
    shape = (SECTIONS, 3, D, INNER)
    base = jnp.clip(jax.random.normal(base_key, shape, jnp.float32), -6.0, 6.0)
    base = base * D ** (-0.5)
    outer = shared_signs(key)[:, :, None] * inner_signs(key)[:, None, :]
    outer = outer * (shared_strength * D ** (-0.5) * INNER ** (-0.5))
    which = jnp.array([1.0, 1.0, 0.0], jnp.float32)[None, :, None, None]
    return (base + which * outer[:, None, :, :]).astype(jnp.bfloat16)


def steps_of(rng, dims, pieces, smallest, largest):
    def one(axis_at, blocks):
        steps = jax.random.uniform(jax.random.fold_in(jax.random.fold_in(rng, 6), axis_at), (blocks,), jnp.float32, smallest / len(pieces), largest / len(pieces))
        return jnp.repeat(jnp.exp(steps), dims[axis_at] // blocks).reshape((-1,) + (1,) * (len(dims) - axis_at - 1))

    level = one(*pieces[0])
    for cut in pieces[1:]:
        level = level * one(*cut)
    return level


def normal_values(key, dims, deviation, limit, shards=(), kind=jnp.bfloat16):
    result = jax.random.normal(key, dims, jnp.float32) * deviation
    if len(shards) > 0:
        result = steps_of(key, dims, shards, -0.22, 0.18) * result
    return jnp.clip(result, min=-limit, max=limit).astype(kind)


def setup_inputs(seed: int = 0) -> dict:
    splits = jax.random.split(jax.random.key(seed), 6)
    tokens = draw_tokens(jax.random.fold_in(splits[5], 71), 0)
    grad_out = normal_values(splits[1], (SECTIONS, NLAT, NLON, D), 1.0, 6.0, ((0, 4), (1, 2), (2, 4)))
    gain = jnp.clip(1.0 + 0.18 * jax.random.normal(splits[2], (SECTIONS, D), jnp.float32), 0.099609375, 1.8984375).astype(jnp.bfloat16)
    w_in = draw_w_in(jax.random.fold_in(splits[5], 71), 0)
    w_out = normal_values(splits[4], (SECTIONS, D, INNER), INNER ** -0.5, 0.21875, ((0, 4), (1, 4)))
    return dict(tokens=tokens, grad_out=grad_out, gain=gain, w_in=w_in, w_out=w_out)


epsilon = 1e-05
masked_score = -1e+30

def neighbour_mask(row_start, total_rows, row_count, col_count):
    ext_rows = row_count + 2 * RADIUS
    ext_cols = col_count + 2 * RADIUS
    cells = jnp.arange(row_count * col_count, dtype=jnp.int32)
    seen = jnp.arange(ext_rows * ext_cols, dtype=jnp.int32)
    query_row = (cells // col_count)[:, None]
    query_col = (cells % col_count)[:, None]
    key_row = (seen // ext_cols)[None, :]
    key_col = (seen % ext_cols)[None, :]
    nearby = (jnp.abs(key_row - query_row - RADIUS) <= RADIUS) & (jnp.abs(key_col - query_col - RADIUS) <= RADIUS)
    global_row = row_start + key_row - RADIUS
    return nearby & (global_row >= 0) & (global_row < total_rows)

def split_heads(array):
    return array.reshape(array.shape[0], HEADS, HEAD).transpose(1, 0, 2)

def join_heads(array):
    return array.transpose(1, 0, 2).reshape(array.shape[1], HEADS * HEAD)

def attend(queries, keys_ext, values_ext, grad_attn, allowed):
    score_scale = HEAD ** (-0.5)

    def one_head(head_parts):
        query_head, key_head, value_head, grad_head = head_parts
        scores = jnp.dot(query_head, key_head.T, preferred_element_type=jnp.float32) * score_scale
        scores = jnp.where(allowed, scores, masked_score)
        maxima = lax.optimization_barrier(jnp.max(scores, axis=1, keepdims=True))
        exponent = jnp.exp(scores - maxima)
        totals = lax.optimization_barrier(jnp.sum(exponent, axis=1, keepdims=True))
        probability = exponent / totals
        grad_prob = jnp.dot(grad_head, value_head.T, preferred_element_type=jnp.float32)
        deltas = lax.optimization_barrier(jnp.sum(probability * grad_prob, axis=1, keepdims=True))
        dscore = (probability * (grad_prob - deltas) * score_scale).astype(jnp.bfloat16)
        grad_query = jnp.dot(dscore, key_head, preferred_element_type=jnp.float32)
        grad_key = jnp.dot(dscore.T, query_head, preferred_element_type=jnp.float32)
        grad_value = jnp.dot(probability.astype(jnp.bfloat16).T, grad_head, preferred_element_type=jnp.float32)
        return (grad_query, grad_key, grad_value)
    return lax.map(one_head, (split_heads(queries), split_heads(keys_ext), split_heads(values_ext), split_heads(grad_attn)))

def section_backward(tokens, grad_out, gain, w_in, w_out):
    lat_cells, lon_cells, feature_width = tokens.shape
    inner_width = w_in.shape[2]
    flat_tokens = tokens.reshape(-1, feature_width).astype(jnp.float32)
    flat_grad = grad_out.reshape(-1, feature_width)
    scale_gain = gain.astype(jnp.float32)
    inverse = lax.rsqrt(lax.optimization_barrier(jnp.mean(flat_tokens * flat_tokens, axis=1, keepdims=True)) + epsilon)
    normed = (flat_tokens * inverse * scale_gain).astype(jnp.bfloat16)
    queries = jnp.dot(normed, w_in[0], preferred_element_type=jnp.float32).astype(jnp.bfloat16)
    keys = jnp.dot(normed, w_in[1], preferred_element_type=jnp.float32).astype(jnp.bfloat16)
    values = jnp.dot(normed, w_in[2], preferred_element_type=jnp.float32).astype(jnp.bfloat16)
    grad_attn = jnp.dot(flat_grad, w_out, preferred_element_type=jnp.float32).astype(jnp.bfloat16)

    def to_grid(array):
        return array.reshape(lat_cells, lon_cells, inner_width)

    def padded(array):
        wrapped = jnp.concatenate([array[:, lon_cells - RADIUS:], array, array[:, :RADIUS]], axis=1)
        return jnp.pad(wrapped, ((RADIUS, RADIUS), (0, 0), (0, 0)))
    query_grid = to_grid(queries)
    grad_grid = to_grid(grad_attn)
    keys_pad = padded(to_grid(keys))
    values_pad = padded(to_grid(values))
    ext_shape = (ROWS_DEV + 2 * RADIUS, COLS_DEV + 2 * RADIUS, inner_width)
    own_shape = (ROWS_DEV, COLS_DEV, inner_width)
    zero_index = jnp.zeros((), jnp.int32)

    def block_step(carried, block_index):
        key_sums, value_sums = carried
        row_start = (block_index // N_LON * ROWS_DEV).astype(jnp.int32)
        col_start = (block_index % N_LON * COLS_DEV).astype(jnp.int32)
        corner = (row_start, col_start, zero_index)
        block_queries = lax.dynamic_slice(query_grid, corner, own_shape).reshape(-1, inner_width)
        block_grads = lax.dynamic_slice(grad_grid, corner, own_shape).reshape(-1, inner_width)
        block_keys = lax.dynamic_slice(keys_pad, corner, ext_shape).reshape(-1, inner_width)
        block_values = lax.dynamic_slice(values_pad, corner, ext_shape).reshape(-1, inner_width)
        allowed = neighbour_mask(row_start, lat_cells, ROWS_DEV, COLS_DEV)
        head_out = attend(block_queries, block_keys, block_values, block_grads, allowed)
        key_part = join_heads(head_out[1]).reshape(ext_shape)
        value_part = join_heads(head_out[2]).reshape(ext_shape)
        key_sums = lax.dynamic_update_slice(key_sums, lax.dynamic_slice(key_sums, corner, ext_shape) + key_part, corner)
        value_sums = lax.dynamic_update_slice(value_sums, lax.dynamic_slice(value_sums, corner, ext_shape) + value_part, corner)
        return ((key_sums, value_sums), join_heads(head_out[0]).astype(jnp.bfloat16))
    sums_shape = (lat_cells + 2 * RADIUS, lon_cells + 2 * RADIUS, inner_width)
    start_sums = (jnp.zeros(sums_shape, jnp.float32), jnp.zeros(sums_shape, jnp.float32))
    (key_sums, value_sums), query_blocks = lax.scan(block_step, start_sums, jnp.arange(N_LAT * N_LON, dtype=jnp.int32))
    grad_query = query_blocks.reshape(N_LAT, N_LON, ROWS_DEV, COLS_DEV, inner_width).transpose(0, 2, 1, 3, 4).reshape(-1, inner_width)

    def folded(sums):
        trimmed = sums[RADIUS:RADIUS + lat_cells]
        middle = trimmed[:, RADIUS:RADIUS + lon_cells]
        middle = middle.at[:, :RADIUS].add(trimmed[:, lon_cells + RADIUS:])
        middle = middle.at[:, lon_cells - RADIUS:].add(trimmed[:, :RADIUS])
        return middle.reshape(-1, inner_width).astype(jnp.bfloat16)
    grad_key = folded(key_sums)
    grad_value = folded(value_sums)
    grad_normed = jnp.dot(grad_query, w_in[0].T, preferred_element_type=jnp.float32)
    grad_normed = grad_normed + jnp.dot(grad_key, w_in[1].T, preferred_element_type=jnp.float32)
    grad_normed = grad_normed + jnp.dot(grad_value, w_in[2].T, preferred_element_type=jnp.float32)
    gained = grad_normed * scale_gain
    mean_term = lax.optimization_barrier(jnp.mean(gained * flat_tokens, axis=1, keepdims=True))
    grad_hidden = (flat_grad.astype(jnp.float32) + inverse * gained - flat_tokens * inverse * inverse * inverse * mean_term).astype(jnp.bfloat16)
    return grad_hidden.reshape(lat_cells, lon_cells, feature_width)

def reference(tokens, grad_out, gain, w_in, w_out):
    hidden = [section_backward(tokens[section_number], grad_out[section_number], gain[section_number], w_in[section_number], w_out[section_number]) for section_number in range(N_SECTION)]
    return jnp.stack(hidden[1:] + hidden[:1])
```

```python
import functools

import jax
import jax.numpy as jnp
from jax import lax
from jax.experimental import pallas as pl
from jax.experimental.pallas import tpu as pltpu
from jax.sharding import PartitionSpec as P

HEADS = 8
HEAD = 96
RADIUS = 6

epsilon = 1e-05
masked_score = -1e30
f32 = jnp.float32
bf16 = jnp.bfloat16
VMEM_LIMIT = 56 * 1024 * 1024


def dot(a, b, dims=((1,), (0,))):
    return lax.dot_general(a, b, (dims, ((), ())), preferred_element_type=f32)


def rotated(block, axis, distance):
    count = lax.axis_size(axis)
    return lax.ppermute(block, axis, [((i + distance) % count, i) for i in range(count)])


def pick(cells, cols, side):
    rows = cells // cols
    out = lax.broadcasted_iota(jnp.int32, (rows * RADIUS, cells), 0)
    src = lax.broadcasted_iota(jnp.int32, (rows * RADIUS, cells), 1)
    first = 0 if side == 0 else cols - RADIUS
    return (src == (out // RADIUS) * cols + out % RADIUS + first).astype(bf16)


def offsets(parts, width):
    if parts == 1:
        return [0]
    me = lax.axis_index("lon")
    return [pl.multiple_of(lax.rem(me + t, parts) * width, 128) for t in range(parts)]


def inverse_rms(x):
    return lax.rsqrt(jnp.mean(x * x, axis=1, keepdims=True) + epsilon)


def keys_kernel(bands, parts, cols, *refs):
    tokens, gain_ref, weights = refs[:bands], refs[bands], refs[bands + 1 : bands + 1 + parts]
    normed_ref, kv_ref, first_ref, last_ref = refs[bands + 1 + parts :]
    gain = gain_ref[...].astype(f32)
    band = tokens[0].shape[0]
    for j in range(bands):
        x = tokens[j][...].astype(f32)
        normed_ref[j * band : (j + 1) * band, :] = (x * inverse_rms(x) * gain).astype(bf16)
    cells = normed_ref.shape[0]
    width = weights[0].shape[1]
    offs = offsets(parts, width)
    pick_first = pick(cells, cols, 0)
    pick_last = pick(cells, cols, 1)
    for m in range(2):
        total = None
        for t in range(parts):
            part = dot(normed_ref[:, pl.ds(offs[t], width)], weights[t][m])
            total = part if total is None else total + part
        rounded = total.astype(bf16)
        kv_ref[m] = rounded
        first_ref[m] = dot(pick_first, rounded).astype(bf16)
        last_ref[m] = dot(pick_last, rounded).astype(bf16)


def allowed_cells(bands, band_rows, cols, query_start, query_count, cells):
    rows = cells // cols
    halo = rows * RADIUS
    lat = lax.axis_index("lat")

    def grid_row(row):
        return lax.rem(lat + row // band_rows, bands) * band_rows + row % band_rows

    query = lax.broadcasted_iota(jnp.int32, (1, query_count), 1) + query_start
    query_row, query_col = grid_row(query // cols), query % cols
    own = lax.broadcasted_iota(jnp.int32, (cells, 1), 0)
    side = lax.broadcasted_iota(jnp.int32, (halo, 1), 0)
    key_row = jnp.concatenate([grid_row(own // cols)] + [grid_row(side // RADIUS)] * 2, axis=0)
    key_col = jnp.concatenate([own % cols, side % RADIUS - RADIUS, side % RADIUS + cols], axis=0)
    return (jnp.abs(key_row - query_row) <= RADIUS) & (jnp.abs(key_col - query_col) <= RADIUS)


def attend_kernel(bands, parts, band_rows, cols, block, *refs):
    normed_ref, grads = refs[0], refs[1 : 1 + bands]
    weights = refs[1 + bands : 1 + bands + parts]
    kv_ref, left_ref, right_ref = refs[1 + bands + parts : 4 + bands + parts]
    gq_ref, gk_ref, gv_ref, to_left_ref, to_right_ref = refs[4 + bands + parts : 9 + bands + parts]
    q_ref, o_ref, keys_ref, values_ref, gk_sum, gv_sum, gqt_ref = refs[9 + bands + parts :]
    scale = HEAD ** (-0.5)
    cells = normed_ref.shape[0]
    band = cells // bands
    halo = left_ref.shape[1]
    width = weights[0].shape[1]
    inner = weights[0].shape[2]
    offs = offsets(parts, width)
    total = None
    for t in range(parts):
        part = dot(normed_ref[:, pl.ds(offs[t], width)], weights[t][0])
        total = part if total is None else total + part
    q_ref[...] = total.astype(bf16)
    for j in range(bands):
        total = None
        for t in range(parts):
            part = dot(grads[j][:, pl.ds(offs[t], width)], weights[t][1])
            total = part if total is None else total + part
        o_ref[j * band : (j + 1) * band, :] = total.astype(bf16)
    for ref, m in ((keys_ref, 0), (values_ref, 1)):
        ref[:cells, :] = kv_ref[m]
        ref[cells : cells + halo, :] = left_ref[m]
        ref[cells + halo :, :] = right_ref[m]
    for start in range(0, cells, block):
        allowed = allowed_cells(bands, band_rows, cols, start, block, cells)
        for lane in range(0, inner, HEAD):
            at = slice(lane, lane + HEAD)
            query = q_ref[start : start + block, at]
            out = o_ref[start : start + block, at]
            key = keys_ref[:, at]
            value = values_ref[:, at]
            scores = dot(key, query, ((1,), (1,))) * scale
            scores = jnp.where(allowed, scores, masked_score)
            maxima = jnp.max(scores, axis=0, keepdims=True)
            exponent = jnp.exp(scores - maxima)
            probability = exponent / jnp.sum(exponent, axis=0, keepdims=True)
            grad_prob = dot(value, out, ((1,), (1,)))
            deltas = jnp.sum(probability * grad_prob, axis=0, keepdims=True)
            dscore = (probability * (grad_prob - deltas) * scale).astype(bf16)
            gqt_ref[at, start : start + block] = dot(key, dscore, ((0,), (0,)))
            grad_key = dot(dscore, query)
            grad_value = dot(probability.astype(bf16), out)
            if start == 0:
                gk_sum[:, at] = grad_key
                gv_sum[:, at] = grad_value
            else:
                gk_sum[:, at] += grad_key
                gv_sum[:, at] += grad_value
    gq_ref[...] = gqt_ref[...].T.astype(bf16)
    gk_ref[...] = gk_sum[:cells, :]
    gv_ref[...] = gv_sum[:cells, :]
    for m, ref in ((0, gk_sum), (1, gv_sum)):
        to_left_ref[m] = ref[cells : cells + halo, :].astype(bf16)
        to_right_ref[m] = ref[cells + halo :, :].astype(bf16)


def hidden_kernel(bands, parts, cols, *refs):
    tokens, grad_ref, gain_ref = refs[:bands], refs[bands], refs[bands + 1]
    kv_weights = refs[bands + 2 : bands + 2 + parts]
    q_weights = refs[bands + 2 + parts : bands + 2 + 2 * parts]
    rest = refs[bands + 2 + 2 * parts :]
    gq_ref, gk_ref, gv_ref, from_left_ref, from_right_ref = rest[:5]
    outs, gn_ref = rest[5 : 5 + bands], rest[5 + bands]
    cells = gq_ref.shape[0]
    band = cells // bands
    width = kv_weights[0].shape[1]
    offs = offsets(parts, width)
    pick_first = pick(cells, cols, 0)
    pick_last = pick(cells, cols, 1)
    grads = [gq_ref[...]]
    for m, ref in ((0, gk_ref), (1, gv_ref)):
        total = ref[...] + dot(pick_first, from_left_ref[m], ((0,), (0,)))
        total = total + dot(pick_last, from_right_ref[m], ((0,), (0,)))
        grads.append(total.astype(bf16))
    for t in range(parts):
        total = dot(grads[0], q_weights[t][0], ((1,), (1,)))
        total = total + dot(grads[1], kv_weights[t][0], ((1,), (1,)))
        total = total + dot(grads[2], kv_weights[t][1], ((1,), (1,)))
        gn_ref[:, pl.ds(offs[t], width)] = total
    gain = gain_ref[...].astype(f32)
    for j in range(bands):
        x = tokens[j][...].astype(f32)
        inverse = inverse_rms(x)
        gained = gn_ref[j * band : (j + 1) * band, :] * gain
        mean_term = jnp.mean(gained * x, axis=1, keepdims=True)
        hidden = inverse * gained - x * (inverse * inverse * inverse * mean_term)
        if j == 0:
            hidden = hidden + grad_ref[...].astype(f32)
        outs[j][...] = hidden.astype(bf16)


def call(kernel, outs, args, scratch=(), flops=0, name=None):
    vmem = pl.BlockSpec(memory_space=pltpu.VMEM)
    moved = sum(a.size * a.dtype.itemsize for a in list(args) + list(outs))
    return pl.pallas_call(
        kernel,
        out_shape=list(outs),
        in_specs=[vmem] * len(args),
        out_specs=[vmem] * len(outs),
        scratch_shapes=list(scratch),
        compiler_params=pltpu.CompilerParams(vmem_limit_bytes=VMEM_LIMIT),
        cost_estimate=pl.CostEstimate(flops=flops, bytes_accessed=moved, transcendentals=0),
        name=name,
    )(*args)


def on_device(tokens, grad_out, gain, w_in, w_out):
    bands = lax.axis_size("lat")
    count = lax.axis_size("lon")
    band_rows, cols, features = tokens.shape[1:]
    inner = w_in.shape[3] // bands
    band = band_rows * cols
    cells = band * bands
    halo = band_rows * bands * RADIUS
    shape = jax.ShapeDtypeStruct
    own_tokens = tokens[0].reshape(band, features)
    own_grads = grad_out[0].reshape(band, features)

    mine = lax.axis_index("lat") * inner
    kv = lax.dynamic_slice_in_dim(w_in[0, 1:], mine, inner, axis=2)
    qo = lax.dynamic_slice_in_dim(jnp.stack([w_in[0, 0], w_out[0]]), mine, inner, axis=2)
    kv_shards, qo_shards = [kv], [qo]
    for _ in range(count - 1):
        kv_shards.append(rotated(kv_shards[-1], "lon", 1))
        qo_shards.append(rotated(qo_shards[-1], "lon", 1))
    all_tokens = [own_tokens] + [rotated(own_tokens, "lat", j) for j in range(1, bands)]
    all_grads = [own_grads] + [rotated(own_grads, "lat", j) for j in range(1, bands)]
    if kv.shape[1] % 128:
        ordered = (jnp.arange(count) - lax.axis_index("lon")) % count

        def joined(shards):
            stacked = jnp.stack(shards)[ordered]
            return [stacked.transpose(1, 0, 2, 3).reshape(2, features, inner)]

        kv_shards, qo_shards = joined(kv_shards), joined(qo_shards)
    parts = len(kv_shards)

    normed, key_value, first, last = call(
        functools.partial(keys_kernel, bands, parts, cols),
        [
            shape((cells, features), bf16),
            shape((2, cells, inner), bf16),
            shape((2, halo, inner), bf16),
            shape((2, halo, inner), bf16),
        ],
        all_tokens + [gain] + kv_shards,
        flops=4 * cells * features * inner,
        name="keys",
    )
    left = rotated(last, "lon", -1)
    right = rotated(first, "lon", 1)
    extent = cells + 2 * halo
    grad_query, grad_key, grad_value, to_left, to_right = call(
        functools.partial(attend_kernel, bands, parts, band_rows, cols, min(cells, 256)),
        [
            shape((cells, inner), bf16),
            shape((cells, inner), f32),
            shape((cells, inner), f32),
            shape((2, halo, inner), bf16),
            shape((2, halo, inner), bf16),
        ],
        [normed] + all_grads + qo_shards + [key_value, left, right],
        scratch=[
            pltpu.VMEM((cells, inner), bf16),
            pltpu.VMEM((cells, inner), bf16),
            pltpu.VMEM((extent, inner), bf16),
            pltpu.VMEM((extent, inner), bf16),
            pltpu.VMEM((extent, inner), f32),
            pltpu.VMEM((extent, inner), f32),
            pltpu.VMEM((inner, cells), f32),
        ],
        flops=4 * cells * features * inner + 10 * cells * extent * inner,
        name="attend",
    )
    from_left = rotated(to_right, "lon", -1)
    from_right = rotated(to_left, "lon", 1)
    partials = call(
        functools.partial(hidden_kernel, bands, parts, cols),
        [shape((band, features), bf16)] * bands,
        all_tokens
        + [own_grads, gain]
        + kv_shards
        + qo_shards
        + [grad_query, grad_key, grad_value, from_left, from_right],
        scratch=[pltpu.VMEM((cells, features), f32)],
        flops=6 * cells * features * inner,
        name="hidden",
    )
    sections = lax.axis_size("section")
    total = None
    for j in range(bands):
        route = [
            (s * bands + l, (s - 1) % sections * bands + (l + j) % bands)
            for s in range(sections)
            for l in range(bands)
        ]
        arrived = lax.ppermute(partials[j], ("section", "lat"), route).astype(f32)
        total = arrived if total is None else total + arrived
    return total.astype(bf16).reshape(1, band_rows, cols, features)


def solution(mesh):
    in_specs = (
        P("section", "lat", "lon", None),
        P("section", "lat", "lon", None),
        P("section", None),
        P("section", None, "lon", None),
        P("section", "lon", None),
    )
    out_specs = P("section", "lat", "lon", None)
    return jax.shard_map(
        on_device, mesh=mesh, in_specs=in_specs, out_specs=out_specs, check_vma=False
    )
```
